32 devices in a mesh: ag: 8 (over y, x, core), tm: 4 (over z).
Axes of the slice: x: 2, y: 2, z: 4, core: 2. Of those that a mesh axis runs over, the one named last changes fastest.
Arguments:
- tokens: bfloat16 [1, 128, 64, 1024], P(None, 'ag', 'tm'), may hold values from -6 to 6
- cotangent: bfloat16 [1, 128, 64, 1024], P(None, 'ag', 'tm'), may hold values from -6 to 6
- observed: int32 [1, 128, 64], replicated, may hold values from 0 to 1, as said below
- time_qkv: bfloat16 [1024, 3072], replicated, may hold values from -12 to 12
- time_out: bfloat16 [1024, 1024], replicated, may hold values from -0.1875 to 0.1875
- agent_qkv: bfloat16 [1024, 3072], replicated, may hold values from -12 to 12
- agent_out: bfloat16 [1024, 1024], replicated, may hold values from -0.1875 to 0.1875
Outputs:
- grad_tokens: bfloat16 [1, 128, 64, 1024], P(None, 'ag', 'tm')
- grad_time_qkv: float32 [1024, 3072], P(('ag', 'tm'))
- grad_time_out: float32 [1024, 1024], P(('ag', 'tm'))
- grad_agent_qkv: float32 [1024, 3072], P(('ag', 'tm'))
- grad_agent_out: float32 [1024, 1024], P(('ag', 'tm'))
The draws below stay inside these ranges and needn't reach their ends.
Inputs may be any that keep to these rules, and one draw needn't show every extreme that they name: 1 marks an observed step of a present agent; each scene's present agents come first, each observed over one run of steps.
All inputs are finite; a program needn't handle non-finite values.
Results may differ from the reference program's by a relative error of at most 0.012.
Values may be sent and summed in bfloat16 or wider, within the bound.
No kernel may reach another device: no remote copies, remote signals or barrier semaphores. Data moves between devices by JAX's collectives and lax.ppermute only.
A program may use at most 192 MiB of HBM per device.

```python
import math
import jax
import jax.numpy as jnp
from jax import lax

D = 1024
H = 16
HD = 64
SCENES = 1
A = 128
STEPS = 64


def draw_observed(key, part):
    first_key, second_key, third_key = jax.random.split(jax.random.fold_in(key, 7), 3)
    present = jax.random.randint(first_key, (SCENES, 1, 1), A // 2, A + 1)
    begin = jax.random.randint(second_key, (SCENES, A, 1), 0, STEPS // 2)
    span = jax.random.randint(third_key, (SCENES, A, 1), STEPS // 4, STEPS + 1)
    agent_ids = jnp.arange(A)[None, :, None]
    step_ids = jnp.arange(STEPS)[None, None, :]
    keep = (agent_ids < present) & (step_ids >= begin) & (step_ids < begin + span)
    return keep.astype(jnp.int32)


def projection_weight(key):
    bound = 6.0 / math.sqrt(D)
    matrix = jnp.clip(jax.random.normal(key, (D, 3 * D), jnp.float32) / math.sqrt(D), -bound, bound)
    return jnp.clip(matrix, -12.0, 12.0).astype(jnp.bfloat16)


def draw_time_qkv(key, part):
    return projection_weight(jax.random.fold_in(key, 11))


def draw_agent_qkv(key, part):
    return projection_weight(jax.random.fold_in(key, 12))


def shard_levels(own_key, dims, cuts, low, top_value):
    def one(axis_at, parts):
        steps = jax.random.uniform(jax.random.fold_in(jax.random.fold_in(own_key, 6), axis_at), (parts,), jnp.float32, low / len(cuts), top_value / len(cuts))
        return jnp.repeat(jnp.exp(steps), dims[axis_at] // parts).reshape((-1,) + (1,) * (len(dims) - axis_at - 1))

    gain = one(*cuts[0])
    for cut in cuts[1:]:
        gain = gain * one(*cut)
    return gain


def bell_draw(own_key, dims, width, most, cuts=(), dtype=jnp.bfloat16):
    values = jax.random.normal(own_key, dims, jnp.float32) * width
    if len(cuts) > 0:
        values = shard_levels(own_key, dims, cuts, -0.22, 0.18) * values
    return jnp.clip(values, min=-most, max=most).astype(dtype)


def setup_inputs(seed: int = 0) -> dict:
    keys = jax.random.split(jax.random.key(seed), 8)
    tokens = bell_draw(keys[0], (SCENES, A, STEPS, D), 1.0, 6.0, ((1, 8), (2, 4)))
    cotangent = bell_draw(keys[1], (SCENES, A, STEPS, D), 1.0, 6.0, ((1, 8), (2, 4)))
    observed = draw_observed(jax.random.fold_in(keys[7], 71), 0)
    time_qkv = draw_time_qkv(jax.random.fold_in(keys[7], 71), 0)
    time_out = bell_draw(keys[4], (D, D), D ** -0.5, 0.1875)
    agent_qkv = draw_agent_qkv(jax.random.fold_in(keys[7], 71), 0)
    agent_out = bell_draw(keys[6], (D, D), D ** -0.5, 0.1875)
    return dict(tokens=tokens, cotangent=cotangent, observed=observed, time_qkv=time_qkv, time_out=time_out, agent_qkv=agent_qkv, agent_out=agent_out)


epsilon = 1e-06
masked_score = -1e+30

def normalize(token_rows):
    widened = token_rows.astype(jnp.float32)
    inverse = lax.rsqrt(lax.optimization_barrier(jnp.mean(widened * widened, axis=-1, keepdims=True)) + epsilon)
    return (widened * inverse, inverse)

def head_split(merged_qkv, which_part):
    batch_size, length, across = merged_qkv.shape[:3]
    member = merged_qkv[..., which_part * D:(which_part + 1) * D]
    return member.reshape(batch_size, length, across, H, HD).astype(jnp.float32)

def allowed_pairs(observed):
    key_seen = jnp.transpose(observed, (0, 2, 1))[:, :, None, :] > 0
    length = observed.shape[1]
    same_slot = jnp.arange(length)[:, None] == jnp.arange(length)[None, :]
    return key_seen | same_slot

def attention_probs(merged_qkv, allowed):
    queries = head_split(merged_qkv, 0)
    keys_part = head_split(merged_qkv, 1)
    scores = jnp.einsum('bqche,bkche->bchqk', queries, keys_part) * HD ** (-0.5)
    scores = jnp.where(allowed[:, :, None], scores, masked_score)
    shifted = jnp.exp(scores - lax.optimization_barrier(jnp.max(scores, axis=-1, keepdims=True)))
    return shifted / lax.optimization_barrier(jnp.sum(shifted, axis=-1, keepdims=True))

def attention_forward(merged_qkv, allowed):
    probability = attention_probs(merged_qkv, allowed)
    rounded = lax.optimization_barrier(probability.astype(jnp.bfloat16)).astype(jnp.float32)
    values_part = head_split(merged_qkv, 2)
    mixed_heads = jnp.einsum('bchqk,bkche->bqche', rounded, values_part)
    batch_size, length, across = merged_qkv.shape[:3]
    return mixed_heads.reshape(batch_size, length, across, D).astype(jnp.bfloat16)

def attention_backward(merged_qkv, allowed, grad_mixed):
    probability = attention_probs(merged_qkv, allowed)
    rounded = lax.optimization_barrier(probability.astype(jnp.bfloat16)).astype(jnp.float32)
    queries = head_split(merged_qkv, 0)
    keys_part = head_split(merged_qkv, 1)
    values_part = head_split(merged_qkv, 2)
    batch_size, length, across = merged_qkv.shape[:3]
    grad_heads = grad_mixed.reshape(batch_size, length, across, H, HD).astype(jnp.float32)
    grad_probs = jnp.einsum('bqche,bkche->bchqk', grad_heads, values_part)
    grad_values = jnp.einsum('bchqk,bqche->bkche', rounded, grad_heads)
    grad_scores = probability * (grad_probs - lax.optimization_barrier(jnp.sum(grad_probs * probability, axis=-1, keepdims=True))) * HD ** (-0.5)
    grad_scores = lax.optimization_barrier(grad_scores.astype(jnp.bfloat16)).astype(jnp.float32)
    grad_queries = jnp.einsum('bchqk,bkche->bqche', grad_scores, keys_part)
    grad_keys = jnp.einsum('bchqk,bqche->bkche', grad_scores, queries)
    joined = jnp.concatenate([member.reshape(batch_size, length, across, D) for member in (grad_queries, grad_keys, grad_values)], axis=-1)
    return joined.astype(jnp.bfloat16)

def project_in(tokens_view, weight_qkv):
    normed, inverse = normalize(tokens_view)
    unit_rows = normed.astype(jnp.bfloat16)
    merged_qkv = jnp.dot(unit_rows.reshape(-1, D), weight_qkv, preferred_element_type=jnp.float32).astype(jnp.bfloat16)
    return (normed, inverse, unit_rows, merged_qkv.reshape(tokens_view.shape[:3] + (3 * D,)))

def sublayer_forward(tokens_view, weight_qkv, weight_out, allowed):
    normed, inverse, unit_rows, merged_qkv = project_in(tokens_view, weight_qkv)
    mixed_heads = attention_forward(merged_qkv, allowed)
    update = jnp.dot(mixed_heads.reshape(-1, D), weight_out, preferred_element_type=jnp.float32).reshape(tokens_view.shape)
    return (tokens_view.astype(jnp.float32) + update).astype(jnp.bfloat16)

def sublayer_backward(tokens_view, weight_qkv, weight_out, allowed, upstream):
    normed, inverse, unit_rows, merged_qkv = project_in(tokens_view, weight_qkv)
    mixed_heads = attention_forward(merged_qkv, allowed)
    flat_up = upstream.reshape(-1, D)
    grad_mixed = jnp.dot(flat_up, weight_out.T, preferred_element_type=jnp.float32).astype(jnp.bfloat16).reshape(tokens_view.shape)
    grad_out = jnp.dot(mixed_heads.reshape(-1, D).T, flat_up, preferred_element_type=jnp.float32)
    grad_merged = attention_backward(merged_qkv, allowed, grad_mixed).reshape(-1, 3 * D)
    grad_qkv = jnp.dot(unit_rows.reshape(-1, D).T, grad_merged, preferred_element_type=jnp.float32)
    grad_unit = jnp.dot(grad_merged, weight_qkv.T, preferred_element_type=jnp.float32).reshape(tokens_view.shape)
    grad_rows = inverse * (grad_unit - normed * lax.optimization_barrier(jnp.mean(grad_unit * normed, axis=-1, keepdims=True)))
    grad_input = (upstream.astype(jnp.float32) + grad_rows).astype(jnp.bfloat16)
    return (grad_input, grad_qkv, grad_out)

def reference(tokens, cotangent, observed, time_qkv, time_out, agent_qkv, agent_out):
    seq_block = 16
    time_blocks = SCENES * A // seq_block
    time_tokens = tokens.reshape(time_blocks, seq_block, STEPS, 1, D)
    time_seen = observed.reshape(time_blocks, seq_block, STEPS, 1)

    def time_forward(block_args):
        return sublayer_forward(block_args[0], time_qkv, time_out, allowed_pairs(block_args[1]))
    first_out = lax.map(time_forward, (time_tokens, time_seen)).reshape(SCENES, A, STEPS, D)
    step_block = 8
    agent_blocks = STEPS // step_block
    agent_first = jnp.moveaxis(first_out.reshape(SCENES, A, agent_blocks, step_block, D), 2, 0)
    agent_up = jnp.moveaxis(cotangent.reshape(SCENES, A, agent_blocks, step_block, D), 2, 0)
    agent_seen = jnp.moveaxis(observed.reshape(SCENES, A, agent_blocks, step_block), 2, 0)
    zero_qkv = jnp.zeros((D, 3 * D), jnp.float32)
    zero_out = jnp.zeros((D, D), jnp.float32)

    def agent_step(running, block_args):
        grad_input, grad_qkv, grad_out = sublayer_backward(block_args[0], agent_qkv, agent_out, allowed_pairs(block_args[2]), block_args[1])
        return ((running[0] + grad_qkv, running[1] + grad_out), grad_input)
    agent_sums, grad_first = lax.scan(agent_step, (zero_qkv, zero_out), (agent_first, agent_up, agent_seen))
    grad_first = jnp.moveaxis(grad_first, 0, 2).reshape(time_blocks, seq_block, STEPS, 1, D)

    def time_step(running, block_args):
        grad_input, grad_qkv, grad_out = sublayer_backward(block_args[0], time_qkv, time_out, allowed_pairs(block_args[2]), block_args[1])
        return ((running[0] + grad_qkv, running[1] + grad_out), grad_input)
    time_sums, grad_input = lax.scan(time_step, (zero_qkv, zero_out), (time_tokens, grad_first, time_seen))
    grad_tokens = grad_input.reshape(SCENES, A, STEPS, D)
    return (grad_tokens, time_sums[0], time_sums[1], agent_sums[0], agent_sums[1])
```

```python
import functools

import jax
import jax.numpy as jnp
from jax import lax
from jax.experimental import pallas as pl
from jax.experimental.pallas import tpu as pltpu
from jax.sharding import PartitionSpec as P

HD = 64
BLOCK = 256

epsilon = 1e-06
masked_score = -1e30


def dot(left, right, left_dim=1, right_dim=0):
    return lax.dot_general(
        left,
        right,
        (((left_dim,), (right_dim,)), ((), ())),
        preferred_element_type=jnp.float32,
    )


def iota(shape, dim):
    return lax.broadcasted_iota(jnp.int32, shape, dim)


def row_order(kind, dims, shape, dim):
    rows = iota(shape, dim)
    if kind == "time":
        return (rows // dims["steps"]) % dims["agents"]
    return rows % dims["sub"]


def leaving_order(dims, tokens):
    leaving = iota((tokens, tokens), 0)
    arriving = iota((tokens, tokens), 1)
    sub = leaving % dims["sub"]
    agent = (leaving // dims["sub"]) % dims["agents"]
    device = leaving // (dims["sub"] * dims["agents"])
    time_at = device % dims["tm"]
    agent_at = device // dims["tm"]
    source = (time_at * dims["agents"] + agent) * dims["steps"] + agent_at * dims["sub"] + sub
    return (source == arriving).astype(jnp.bfloat16)


def score_bias(kind, dims, seen):
    tokens = seen.shape[1]
    same = row_order(kind, dims, (tokens, tokens), 0) == row_order(kind, dims, (tokens, tokens), 1)
    own = iota((tokens, tokens), 0) == iota((tokens, tokens), 1)
    allowed = same & ((seen > 0) | own)
    return jnp.where(allowed, 0.0, masked_score)


def unit_rows(x):
    widened = x.astype(jnp.float32)
    inverse = lax.rsqrt(jnp.mean(widened * widened, axis=-1, keepdims=True) + epsilon)
    return widened * inverse, inverse


def softmax_rows(scores, bias):
    scores = scores * HD ** (-0.5) + bias
    shifted = jnp.exp(scores - jnp.max(scores, axis=-1, keepdims=True))
    return shifted * (1.0 / jnp.sum(shifted, axis=-1, keepdims=True))


def head_lane(head, width):
    lanes = iota((1, width), 1) // HD
    return (lanes == head).astype(jnp.float32).astype(jnp.bfloat16)


def forward_kernel(kind, dims, x_ref, seen_ref, wq_ref, wk_ref, wv_ref, wo_ref, out_ref, unit_ref, bias_ref, acc_ref):
    step = pl.program_id(0)

    @pl.when(step == 0)
    def _():
        unit_ref[...] = unit_rows(x_ref[...])[0].astype(jnp.bfloat16)
        bias_ref[...] = score_bias(kind, dims, seen_ref[...])
        acc_ref[...] = x_ref[...].astype(jnp.float32)

    unit = unit_ref[...]
    queries = dot(unit, wq_ref[...]).astype(jnp.bfloat16)
    keys = dot(unit, wk_ref[...]).astype(jnp.bfloat16)
    values = dot(unit, wv_ref[...]).astype(jnp.bfloat16)
    width = queries.shape[1]
    mixed = jnp.zeros(queries.shape, jnp.float32)
    for head in range(width // HD):
        lane = head_lane(head, width)
        prob = softmax_rows(dot(queries * lane, keys, 1, 1), bias_ref[...])
        mixed += dot(prob.astype(jnp.bfloat16), values * lane)
    acc_ref[...] += dot(mixed.astype(jnp.bfloat16), wo_ref[...])

    @pl.when(step == pl.num_programs(0) - 1)
    def _():
        rounded = acc_ref[...].astype(jnp.bfloat16)
        out_ref[...] = dot(leaving_order(dims, rounded.shape[0]), rounded).astype(jnp.bfloat16)


def backward_kernel(kind, dims, x_ref, g_ref, seen_ref, wq_ref, wk_ref, wv_ref, wo_ref, grad_ref, unit_ref, up_ref, merged_ref, mixed_ref, bias_ref, acc_ref):
    step = pl.program_id(0)

    @pl.when(step == 0)
    def _():
        unit_ref[...] = unit_rows(x_ref[...])[0].astype(jnp.bfloat16)
        bias_ref[...] = score_bias(kind, dims, seen_ref[...])
        acc_ref[...] = jnp.zeros(acc_ref.shape, jnp.float32)
        if kind == "time":
            order = leaving_order(dims, x_ref.shape[0])
            up_ref[...] = dot(order, g_ref[...], 0, 0).astype(jnp.bfloat16)
        else:
            up_ref[...] = g_ref[...]

    unit = unit_ref[...]
    queries = dot(unit, wq_ref[...]).astype(jnp.bfloat16)
    keys = dot(unit, wk_ref[...]).astype(jnp.bfloat16)
    values = dot(unit, wv_ref[...]).astype(jnp.bfloat16)
    grad_mixed = dot(up_ref[...], wo_ref[...], 1, 1).astype(jnp.bfloat16)
    width = queries.shape[1]
    zero = jnp.zeros(queries.shape, jnp.float32)
    mixed, grad_q, grad_k, grad_v = zero, zero, zero, zero
    for head in range(width // HD):
        lane = head_lane(head, width)
        q_head = queries * lane
        g_head = grad_mixed * lane
        prob = softmax_rows(dot(q_head, keys, 1, 1), bias_ref[...])
        rounded = prob.astype(jnp.bfloat16)
        grad_prob = dot(g_head, values, 1, 1)
        mixed += dot(rounded, values * lane)
        grad_v += dot(rounded, g_head, 0, 0)
        inner = jnp.sum(grad_prob * prob, axis=-1, keepdims=True)
        grad_scores = (prob * (grad_prob - inner) * HD ** (-0.5)).astype(jnp.bfloat16)
        grad_q += dot(grad_scores, keys * lane)
        grad_k += dot(grad_scores, q_head, 0, 0)
    model = x_ref.shape[1]
    at = pl.multiple_of(step * width, width)
    mixed_ref[:, pl.ds(at, width)] = mixed.astype(jnp.bfloat16)
    for part, (value, weight_ref) in enumerate(((grad_q, wq_ref), (grad_k, wk_ref), (grad_v, wv_ref))):
        value = value.astype(jnp.bfloat16)
        merged_ref[:, pl.ds(pl.multiple_of(part * model + step * width, width), width)] = value
        acc_ref[...] += dot(value, weight_ref[...], 1, 1)

    @pl.when(step == pl.num_programs(0) - 1)
    def _():
        normed, inverse = unit_rows(x_ref[...])
        grad_unit = acc_ref[...]
        inner = jnp.mean(grad_unit * normed, axis=-1, keepdims=True)
        grad_rows = inverse * (grad_unit - normed * inner)
        grad_ref[...] = (up_ref[...].astype(jnp.float32) + grad_rows).astype(jnp.bfloat16)


def weight_specs(model):
    parts = model // BLOCK
    return [
        pl.BlockSpec((model, BLOCK), lambda i: (0, i)),
        pl.BlockSpec((model, BLOCK), lambda i: (0, parts + i)),
        pl.BlockSpec((model, BLOCK), lambda i: (0, 2 * parts + i)),
        pl.BlockSpec((BLOCK, model), lambda i: (i, 0)),
    ]


def whole(shape):
    return pl.BlockSpec(shape, lambda i: (0,) * len(shape))


def sublayer_forward(kind, dims, x, seen, w_qkv, w_out):
    tokens, model = x.shape
    return pl.pallas_call(
        functools.partial(forward_kernel, kind, dims),
        name="sublayer_forward",
        grid=(model // BLOCK,),
        in_specs=[whole(x.shape), whole(seen.shape)] + weight_specs(model),
        out_specs=whole(x.shape),
        out_shape=jax.ShapeDtypeStruct(x.shape, jnp.bfloat16),
        scratch_shapes=[
            pltpu.VMEM((tokens, model), jnp.bfloat16),
            pltpu.VMEM((tokens, tokens), jnp.float32),
            pltpu.VMEM((tokens, model), jnp.float32),
        ],
        compiler_params=pltpu.CompilerParams(dimension_semantics=("arbitrary",)),
    )(x, seen, w_qkv, w_qkv, w_qkv, w_out)


def sublayer_backward(kind, dims, x, upstream, seen, w_qkv, w_out):
    tokens, model = x.shape
    rows = jax.ShapeDtypeStruct(x.shape, jnp.bfloat16)
    merged = jax.ShapeDtypeStruct((tokens, 3 * model), jnp.bfloat16)
    return pl.pallas_call(
        functools.partial(backward_kernel, kind, dims),
        name="sublayer_backward",
        grid=(model // BLOCK,),
        in_specs=[whole(x.shape), whole(x.shape), whole(seen.shape)] + weight_specs(model),
        out_specs=[whole(x.shape), whole(x.shape), whole(x.shape), whole(merged.shape), whole(x.shape)],
        out_shape=[rows, rows, rows, merged, rows],
        scratch_shapes=[
            pltpu.VMEM((tokens, tokens), jnp.float32),
            pltpu.VMEM((tokens, model), jnp.float32),
        ],
        compiler_params=pltpu.CompilerParams(dimension_semantics=("arbitrary",)),
    )(x, upstream, seen, w_qkv, w_qkv, w_qkv, w_out)


def flip(value, axis, bit):
    size = lax.axis_size(axis)
    return lax.ppermute(value, axis, [(i, i ^ bit) for i in range(size)])


def axis_bits(axis):
    bits = []
    bit = lax.axis_size(axis) // 2
    while bit:
        bits.append((axis, bit))
        bit //= 2
    return bits


def halve(value, bits, order):
    left = list(bits)
    for axis, bit in order:
        at = left.index((axis, bit))
        mine = (lax.axis_index(axis) // bit) % 2
        sent = lax.dynamic_index_in_dim(value, 1 - mine, at, keepdims=False)
        kept = lax.dynamic_index_in_dim(value, mine, at, keepdims=False)
        got = flip(sent.astype(jnp.bfloat16), axis, bit)
        value = kept + got.astype(jnp.float32)
        left.pop(at)
    return value


def pair_columns(value, which):
    tokens, model = value.shape
    split = value.reshape(tokens, lax.axis_size("ag") // 2, 2, model // lax.axis_size("ag"))
    return lax.dynamic_index_in_dim(split, which, 2, keepdims=False).reshape(tokens, model // 2)


def weight_sums(unit, merged, mixed, upstream):
    core = lax.axis_index("ag") % 2
    share = lambda value: flip(value, "ag", 1)
    up_other = share(upstream)
    mixed_other = share(pair_columns(mixed, 1 - core))
    merged_other = share(merged)
    unit_other = share(pair_columns(unit, 1 - core))
    unit_own = pair_columns(unit, core)
    mixed_own = pair_columns(mixed, core)
    ag_bits, tm_bits = axis_bits("ag")[:-1], axis_bits("tm")
    bits = ag_bits + tm_bits
    heads = (2,) * len(bits)
    half = merged.shape[1] // 2

    def product(left, left_other, right, right_other):
        value = dot(left, right, 0, 0) + dot(left_other, right_other, 0, 0)
        return value.reshape(heads + (value.shape[0] >> len(bits), value.shape[1]))

    out = halve(product(mixed_own, mixed_other, upstream, up_other), bits, tm_bits[::-1] + ag_bits[::-1])
    one = product(unit_own, unit_other, merged[:, :half], merged_other[:, :half])
    two = product(unit_own, unit_other, merged[:, half:], merged_other[:, half:])
    one = halve(one, bits, ag_bits[::-1] + tm_bits[::-1])
    two = halve(two, bits, ag_bits + tm_bits[::-1])
    return jnp.concatenate([one, two], axis=1), out


def exchange(value, axes):
    size = 1
    for axis in axes:
        size *= lax.axis_size(axis)
    tokens, model = value.shape
    blocks = value.reshape(size, tokens // size, model)
    axes = axes if len(axes) > 1 else axes[0]
    return lax.all_to_all(blocks, axes, split_axis=0, concat_axis=0, tiled=True).reshape(tokens, model)


def local(tokens, cotangent, observed, time_qkv, time_out, agent_qkv, agent_out):
    ag, tm = lax.axis_size("ag"), lax.axis_size("tm")
    agent_at, time_at = lax.axis_index("ag"), lax.axis_index("tm")
    scenes, agents, steps, model = tokens.shape
    assert scenes == 1
    count = agents * steps
    dims = {"ag": ag, "tm": tm, "agents": agents // tm, "steps": steps, "sub": steps // ag}

    seen_time = lax.dynamic_slice_in_dim(observed[0], agent_at * agents + time_at * dims["agents"], dims["agents"], 0)
    seen_time = seen_time.reshape(dims["agents"], tm, steps).transpose(1, 0, 2).reshape(1, count)
    seen_agent = lax.dynamic_slice_in_dim(observed[0], time_at * steps + agent_at * dims["sub"], dims["sub"], 1)
    seen_agent = seen_agent.reshape(1, count)

    x_time = exchange(tokens.reshape(count, model), ("tm",))
    up = cotangent.reshape(agents, ag, dims["sub"], model).transpose(1, 0, 2, 3).reshape(count, model)
    up_agent = exchange(up, ("ag",))
    first = sublayer_forward("time", dims, x_time, seen_time, time_qkv, time_out)
    x_agent = exchange(first, ("ag", "tm"))
    grad_first, unit, up, merged, mixed = sublayer_backward("agent", dims, x_agent, up_agent, seen_agent, agent_qkv, agent_out)
    up_time = exchange(grad_first, ("ag", "tm"))
    agent_sums = weight_sums(unit, merged, mixed, up)
    grad_time, unit, up, merged, mixed = sublayer_backward("time", dims, x_time, up_time, seen_time, time_qkv, time_out)
    grad_tokens = exchange(grad_time, ("tm",)).reshape(tokens.shape)
    time_sums = weight_sums(unit, merged, mixed, up)
    return (grad_tokens,) + time_sums + agent_sums


def solution(mesh):
    in_specs = (P(None, "ag", "tm", None), P(None, "ag", "tm", None), P(), P(), P(), P(), P())
    out_specs = (
        P(None, "ag", "tm", None),
        P(("ag", "tm"), None),
        P(("ag", "tm"), None),
        P(("ag", "tm"), None),
        P(("ag", "tm"), None),
    )
    return jax.shard_map(local, mesh=mesh, in_specs=in_specs, out_specs=out_specs, check_vma=False)
```
